32 devices in a mesh: groups: 2 (over y), patch: 8 (over z, x), head: 2 (over core).
Axes of the slice: x: 2, y: 2, z: 4, core: 2. Of those that a mesh axis runs over, the one named last changes fastest.
Arguments:
- queries: bfloat16 [2, 256, 1536], P(None, ('groups', 'patch'), 'head'), parts along dimension 1, may hold values from -15 to 15
- stale_pairs: bfloat16 [2, 320, 1536], P(None, ('groups', 'patch'), 'head'), parts along dimension 1, may hold values from -6 to 6
- step_pairs: bfloat16 [2, 2, 320, 1536], P(None, None, ('groups', 'patch'), 'head'), parts along dimension 2, may hold values from -6 to 6
- hidden: bfloat16 [256, 3072], P(('groups', 'patch'), 'head'), parts along dimension 0, may hold values from -3 to 3
- out_weight: bfloat16 [1536, 3072], P('head'), may hold values from -0.15625 to 0.15625
- gate_table: bfloat16 [28, 3072], replicated, may hold values from -4 to 4
- t_index: int32 [4], P('groups'), parts along dimension 0, may hold values from 0 to 27
- text_len: int32 [2], P('groups'), parts along dimension 0, may hold values from 1 to 32
Outputs:
- final_latents: bfloat16 [256, 3072], P(('groups', 'patch', 'head')), parts along dimension 0
The draws below stay inside these ranges and needn't reach their ends.
There are 2 independent parts, one for each index of `groups`. The reference program is written for one: setup_inputs(seed, part) draws one part's arguments, and reference() takes and returns one part's arrays. A program takes and returns all parts, laid end to end along the dimension named above; an argument that names none is the same for every part. Nothing has to cross between parts.
All inputs are finite; a program needn't handle non-finite values.
Results may differ from the reference program's by a relative error of at most 0.0065.
Values may be sent and summed in bfloat16 or wider, within the bound.
A program may use at most 128 MiB of HBM per device.

```python
import jax
import jax.numpy as jnp
from jax import lax

D = 3072
HEADS = 12
HDIM = 128
LAT_DEV = 16
TXT_DEV = 4
NSCHED = 28
ROWS = 20
LAT = 128
TXT = 32
SEQ = 160
HD = 1536
N_PATCH = 8


def joint_draw(key):
    base = jax.random.fold_in(key, 7)
    key_query, key_stale, key_fresh = jax.random.split(base, 3)
    queries = 2.5 * jax.random.truncated_normal(key_query, -6.0, 6.0, (2, LAT, HD), jnp.float32)
    stale = jax.random.truncated_normal(key_stale, -6.0, 6.0, (2, SEQ, HD), jnp.float32)
    fresh = jax.random.truncated_normal(key_fresh, -6.0, 6.0, (2, 2, SEQ, HD), jnp.float32)
    return (queries, stale, fresh)


def draw_queries(key, part):
    return joint_draw(key)[0].astype(jnp.bfloat16)


def draw_stale_pairs(key, part):
    return joint_draw(key)[1].astype(jnp.bfloat16)


def draw_step_pairs(key, part):
    return joint_draw(key)[2].astype(jnp.bfloat16)


def levels(key, shape, pieces, least, top_value):
    def one(position, shards_of):
        heights = jax.random.uniform(jax.random.fold_in(jax.random.fold_in(key, 6), position), (shards_of,), jnp.float32, least / len(pieces), top_value / len(pieces))
        return jnp.repeat(jnp.exp(heights), shape[position] // shards_of).reshape((-1,) + (1,) * (len(shape) - position - 1))

    gain = one(*pieces[0])
    for cut in pieces[1:]:
        gain = gain * one(*cut)
    return gain


def noise(rng, shape, width, bound, cuts=(), held_as=jnp.bfloat16):
    factor_of = levels(rng, shape, cuts, -0.22, 0.18) if cuts else 1.0
    entries = jax.random.normal(rng, shape, jnp.float32) * width * factor_of
    return jnp.minimum(jnp.maximum(entries, -bound), bound).astype(held_as)


def setup_inputs(seed: int = 0, part: int = 0) -> dict:
    splits = jax.random.split(jax.random.key(seed), 9)
    part_splits = jax.random.split(jax.random.fold_in(splits[8], part), 9)
    return {
        "queries": draw_queries(jax.random.fold_in(jax.random.fold_in(splits[8], part), 71), part),
        "stale_pairs": draw_stale_pairs(jax.random.fold_in(jax.random.fold_in(splits[8], part), 71), part),
        "step_pairs": draw_step_pairs(jax.random.fold_in(jax.random.fold_in(splits[8], part), 71), part),
        "hidden": noise(part_splits[3], (LAT, D), 0.5, 3.0, ((0, 8), (1, 2))),
        "out_weight": noise(splits[4], (HD, D), HD ** -0.5, 0.15625, ((0, 2),)),
        "gate_table": noise(splits[5], (NSCHED, D), 1.0, 4.0),
        "t_index": jax.random.randint(part_splits[6], (2,), 0, NSCHED).astype(jnp.int32),
        "text_len": jax.random.randint(part_splits[7], (1,), 1, TXT + 1).astype(jnp.int32),
    }


def attend(query_rows, key_rows, value_rows, usable):
    count = query_rows.shape[0]
    total = key_rows.shape[0]
    qf = query_rows.reshape(count, HEADS, HDIM).astype(jnp.float32)
    kf = key_rows.reshape(total, HEADS, HDIM).astype(jnp.float32)
    vf = value_rows.reshape(total, HEADS, HDIM).astype(jnp.float32)
    scores = jnp.einsum("qhd,khd->hqk", qf, kf) * (1.0 / (HDIM ** 0.5))
    scores = jnp.where(usable[None, None, :], scores, jnp.float32(-1e30))
    top = jnp.max(scores, axis=2, keepdims=True)
    expo = jnp.exp(scores - top)
    weights = (expo / jnp.sum(expo, axis=2, keepdims=True)).astype(jnp.bfloat16)
    mixed = jnp.einsum("hqk,khd->qhd", weights.astype(jnp.float32), vf)
    return mixed.reshape(count, HEADS * HDIM).astype(jnp.bfloat16)


def reference(queries, stale_pairs, step_pairs, hidden, out_weight, gate_table, t_index, text_len):
    positions = jnp.arange(SEQ, dtype=jnp.int32)
    within = positions % ROWS
    holder = positions // ROWS
    usable = (within < LAT_DEV) | (holder * TXT_DEV + within - LAT_DEV < text_len[0])
    state = hidden.astype(jnp.float32)
    remote_sets = (stale_pairs, step_pairs[0])
    for section in range(2):
        remote = remote_sets[section]
        fresh = step_pairs[section]
        section_queries = queries[section]

        def one_strip(strip_index):
            start = (strip_index * ROWS).astype(jnp.int32)
            own = lax.dynamic_slice_in_dim(fresh, start, ROWS, axis=1)
            pairs = lax.dynamic_update_slice_in_dim(remote, own, start, axis=1)
            qstart = (strip_index * LAT_DEV).astype(jnp.int32)
            query_rows = lax.dynamic_slice_in_dim(section_queries, qstart, LAT_DEV, axis=0)
            return attend(query_rows, pairs[0], pairs[1], usable)

        attended = lax.map(one_strip, jnp.arange(N_PATCH, dtype=jnp.int32)).reshape(LAT, HD)
        projected = jnp.dot(attended, out_weight, preferred_element_type=jnp.float32)
        gate_row = gate_table[t_index[section]].astype(jnp.float32)
        state = state + gate_row[None, :] * projected
    return state.astype(jnp.bfloat16)
```

```python
import functools

import jax
import jax.numpy as jnp
from jax import lax
from jax.experimental import pallas as pl
from jax.experimental.pallas import tpu as pltpu
from jax.sharding import PartitionSpec as P

HDIM = 128
PAD = 32
MESH_ID = pl.DeviceIdType.MESH


def minor_extent(mesh):
    names = list(mesh.axis_names)
    order = [names.index("patch")] + [i for i, name in enumerate(names) if name != "patch"]
    line = mesh.devices.transpose(order).reshape(mesh.shape["patch"], -1)[:, 0]
    count = len(line)
    try:
        spots = [tuple(device.coords) for device in line]
    except AttributeError:
        return 2 if count % 2 == 0 else 1
    varying = lambda spot: [i for i in range(len(spot)) if spot[i] != spots[0][i]]
    extent = 1
    while extent < count and varying(spots[extent]) == varying(spots[1]) and len(varying(spots[1])) == 1:
        extent += 1
    return extent if count % extent == 0 else 1


def kernel(
    major, minor, heads_split,
    t_ref, len_ref, q_hbm, stale_hbm, step_hbm, hid_hbm, w_hbm, gate_hbm,
    out_ref,
    slots, padded, w_v, q_v, hid_v, gate_v, mixed, partial, arrived,
    load_sem, send_sem, recv_sem, swap_send, swap_recv,
):
    count = major * minor
    me = lax.axis_index("patch")
    mine = lax.axis_index("head")
    a, b = me // minor, me % minor
    strip_rows = stale_hbm.shape[1]
    lat_rows = q_hbm.shape[1]
    text_rows = strip_rows - lat_rows
    feats = q_hbm.shape[2]
    width = w_hbm.shape[1]
    col_width = hid_hbm.shape[1]
    out_rows = lat_rows // heads_split
    sides = (
        (a > 0, me - minor), (a < major - 1, me + minor),
        (b > 0, me - 1), (b < minor - 1, me + 1),
    )
    if minor == 1:
        sides = sides[:2]

    loads = [
        pltpu.make_async_copy(step_hbm.at[0], slots.at[me, 0], load_sem.at[0]),
        pltpu.make_async_copy(step_hbm.at[1], slots.at[me, 1], load_sem.at[1]),
        pltpu.make_async_copy(q_hbm, q_v, load_sem.at[2]),
        pltpu.make_async_copy(hid_hbm, hid_v, load_sem.at[3]),
        pltpu.make_async_copy(gate_hbm, gate_v, load_sem.at[4]),
        pltpu.make_async_copy(w_hbm, w_v, load_sem.at[5]),
    ]
    barrier = pltpu.get_barrier_semaphore()
    greeted = heads_split - 1
    for there, index in sides:
        greeted = greeted + there.astype(jnp.int32)

        @pl.when(there)
        def _():
            pl.semaphore_signal(barrier, inc=1, device_id={"patch": index}, device_id_type=MESH_ID)

    for k in range(1, heads_split):
        pl.semaphore_signal(
            barrier, inc=1, device_id={"head": (mine + k) % heads_split}, device_id_type=MESH_ID
        )
    for load in loads:
        load.start()
    pl.semaphore_wait(barrier, greeted)

    def remote(source, block, piece, side):
        return pltpu.make_async_remote_copy(
            src_ref=source,
            dst_ref=slots.at[block, piece],
            send_sem=send_sem.at[block, piece, side],
            recv_sem=recv_sem.at[block, piece],
            device_id={"patch": sides[side][1]},
            device_id_type=MESH_ID,
        )

    def spread(source, block, piece, to):
        for side in to:
            if side < len(sides):
                @pl.when(sides[side][0])
                def _():
                    remote(source, block, piece, side).start()

    def drain(block, piece, to):
        for side in to:
            if side < len(sides):
                @pl.when(sides[side][0])
                def _():
                    remote(slots.at[block, piece], block, piece, side).wait_send()

    def landed(block, piece):
        remote(slots.at[block, piece], block, piece, 0).wait_recv()

    own_source = (stale_hbm, step_hbm.at[0])
    for piece in range(2):
        spread(own_source[piece], me, piece, (0, 1, 2, 3))

    padded[...] = jnp.zeros_like(padded)
    loads[4].wait()
    plan_rows = lax.broadcasted_iota(jnp.int32, gate_v.shape, 0)
    table = gate_v[...].astype(jnp.float32)
    gates = [
        jnp.sum(jnp.where(plan_rows == t_ref[s], table, 0.0), axis=0, keepdims=True)
        for s in range(2)
    ]

    for t in range(1, major):
        for piece in range(2):
            for away, onward in ((a - t, 1), (a + t, 0)):
                @pl.when((away >= 0) & (away < major))
                def _():
                    block = away * minor + b
                    landed(block, piece)
                    spread(slots.at[block, piece], block, piece, (onward, 2, 3))

    for u in range(1, minor):
        for away, onward in ((b - u, 3), (b + u, 2)):
            @pl.when((away >= 0) & (away < minor))
            def _():
                def one(r, carry):
                    block = r * minor + away
                    for piece in range(2):
                        landed(block, piece)
                        if u < minor - 1:
                            spread(slots.at[block, piece], block, piece, (onward,))
                    return carry

                lax.fori_loop(0, major, one, 0)

    for load in (loads[0], loads[1], loads[2]):
        load.wait()

    keys = count * PAD
    place = lax.broadcasted_iota(jnp.int32, (1, keys), 1)
    holder, within = place // PAD, place % PAD
    usable = (within < lat_rows) | (
        (within < strip_rows) & (holder * text_rows + within - lat_rows < len_ref[0])
    )

    def attend(s):
        def fill(p, carry):
            start = pl.multiple_of(p * PAD, PAD)
            for kind in range(2):
                padded[kind, pl.ds(start, strip_rows), :] = slots[p, s, kind]
            return carry

        if count <= 8:
            for p in range(count):
                fill(p, 0)
        else:
            lax.fori_loop(0, count, fill, 0)
        for h in range(feats // HDIM):
            cols = slice(h * HDIM, (h + 1) * HDIM)
            scores = lax.dot_general(
                q_v[s, :, cols], padded[0, :, cols], (((1,), (1,)), ((), ())),
                preferred_element_type=jnp.float32,
            ) * (1.0 / HDIM**0.5)
            scores = jnp.where(usable, scores, jnp.float32(-1e30))
            top = jnp.max(scores, axis=1, keepdims=True)
            expo = jnp.exp(scores - top)
            weights = (expo * (1.0 / jnp.sum(expo, axis=1, keepdims=True))).astype(jnp.bfloat16)
            mixed[s, :, cols] = jnp.dot(
                weights, padded[1, :, cols], preferred_element_type=jnp.float32
            ).astype(jnp.bfloat16)

    chunks = 2 * heads_split
    chunk = width // chunks
    swaps = []
    for s in range(2):
        attend(s)
        if s == 0:
            loads[3].wait()
            loads[5].wait()
        for c in range(chunks):
            cols = slice(c * chunk, (c + 1) * chunk)
            term = gates[s][:, cols] * jnp.dot(
                mixed[s], w_v[:, cols], preferred_element_type=jnp.float32
            )
            if s == 0:
                owner, inner = (c * chunk) // col_width, (c * chunk) % col_width
                base = hid_v[:, inner:inner + chunk].astype(jnp.float32)
                partial[:, cols] = jnp.where(mine == owner, base, 0.0) + term
            else:
                partial[:, cols] = partial[:, cols] + term
                for k in range(1, heads_split):
                    peer = (mine + k) % heads_split
                    swap = pltpu.make_async_remote_copy(
                        src_ref=partial.at[pl.ds(pl.multiple_of(peer * out_rows, out_rows), out_rows), pl.ds(c * chunk, chunk)],
                        dst_ref=arrived.at[k - 1, :, pl.ds(c * chunk, chunk)],
                        send_sem=swap_send.at[k - 1, c],
                        recv_sem=swap_recv.at[k - 1, c],
                        device_id={"head": peer},
                        device_id_type=MESH_ID,
                    )
                    swap.start()
                    swaps.append((c, k, swap))

    own = pl.ds(pl.multiple_of(mine * out_rows, out_rows), out_rows)
    for c in range(chunks):
        cols = slice(c * chunk, (c + 1) * chunk)
        total = partial[own, cols]
        for cc, k, swap in swaps:
            if cc == c:
                swap.wait_recv()
                total = total + arrived[k - 1, :, cols]
        out_ref[:, cols] = total.astype(out_ref.dtype)

    for _, _, swap in swaps:
        swap.wait_send()
    for piece in range(2):
        drain(me, piece, (0, 1, 2, 3))
    for t in range(1, major):
        for piece in range(2):
            for away, onward in ((a - t, 1), (a + t, 0)):
                @pl.when((away >= 0) & (away < major))
                def _():
                    drain(away * minor + b, piece, (onward, 2, 3))
    for u in range(1, minor - 1):
        for away, onward in ((b - u, 3), (b + u, 2)):
            @pl.when((away >= 0) & (away < minor))
            def _():
                def one(r, carry):
                    for piece in range(2):
                        drain(r * minor + away, piece, (onward,))
                    return carry

                lax.fori_loop(0, major, one, 0)


def per_device(major, minor, heads_split, queries, stale_pairs, step_pairs, hidden, out_weight, gate_table, t_index, text_len):
    count = major * minor
    lat_rows, feats = queries.shape[1:]
    width = out_weight.shape[1]
    out_rows = lat_rows // heads_split
    chunks = 2 * heads_split
    anywhere = pl.BlockSpec(memory_space=pl.ANY)
    scalars = pl.BlockSpec(memory_space=pltpu.SMEM)
    return pl.pallas_call(
        functools.partial(kernel, major, minor, heads_split),
        out_shape=jax.ShapeDtypeStruct((out_rows, width), jnp.bfloat16),
        in_specs=[scalars] * 2 + [anywhere] * 6,
        out_specs=pl.BlockSpec(memory_space=pltpu.VMEM),
        scratch_shapes=[
            pltpu.VMEM((count,) + step_pairs.shape, jnp.bfloat16),
            pltpu.VMEM((2, count * PAD, feats), jnp.bfloat16),
            pltpu.VMEM(out_weight.shape, jnp.bfloat16),
            pltpu.VMEM(queries.shape, jnp.bfloat16),
            pltpu.VMEM(hidden.shape, jnp.bfloat16),
            pltpu.VMEM(gate_table.shape, jnp.bfloat16),
            pltpu.VMEM(queries.shape, jnp.bfloat16),
            pltpu.VMEM((lat_rows, width), jnp.float32),
            pltpu.VMEM((heads_split - 1, out_rows, width), jnp.float32),
            pltpu.SemaphoreType.DMA((6,)),
            pltpu.SemaphoreType.DMA((count, 2, 4)),
            pltpu.SemaphoreType.DMA((count, 2)),
            pltpu.SemaphoreType.DMA((heads_split - 1, chunks)),
            pltpu.SemaphoreType.DMA((heads_split - 1, chunks)),
        ],
        compiler_params=pltpu.CompilerParams(collective_id=0, has_side_effects=True),
        name="block",
    )(t_index, text_len, queries, stale_pairs, step_pairs, hidden, out_weight, gate_table)


def solution(mesh):
    minor = minor_extent(mesh)
    return jax.shard_map(
        functools.partial(per_device, mesh.shape["patch"] // minor, minor, mesh.shape["head"]),
        mesh=mesh,
        in_specs=(
            P(None, ("groups", "patch"), "head"),
            P(None, ("groups", "patch"), "head"),
            P(None, None, ("groups", "patch"), "head"),
            P(("groups", "patch"), "head"),
            P("head", None),
            P(),
            P("groups"),
            P("groups"),
        ),
        out_specs=P(("groups", "patch", "head"), None),
        check_vma=False,
    )
```

```python
import functools

import jax
import jax.numpy as jnp
from jax import lax
from jax.experimental import pallas as pl
from jax.experimental.pallas import tpu as pltpu
from jax.sharding import PartitionSpec as P

HDIM = 128
PAD = 32
MESH_ID = pl.DeviceIdType.MESH


def minor_extent(mesh):
    names = list(mesh.axis_names)
    order = [names.index("patch")] + [i for i, name in enumerate(names) if name != "patch"]
    line = mesh.devices.transpose(order).reshape(mesh.shape["patch"], -1)[:, 0]
    count = len(line)
    try:
        spots = [tuple(device.coords) for device in line]
    except AttributeError:
        return 2 if count % 2 == 0 else 1
    varying = lambda spot: [i for i in range(len(spot)) if spot[i] != spots[0][i]]
    extent = 1
    while extent < count and varying(spots[extent]) == varying(spots[1]) and len(varying(spots[1])) == 1:
        extent += 1
    return extent if count % extent == 0 else 1


def kernel(
    major, minor, heads_split,
    t_ref, len_ref, q_hbm, stale_hbm, step_hbm, hid_hbm, w_hbm, gate_hbm,
    out_ref,
    slots, own_v, padded, w_v, q_v, hid_v, gate_v, partial, arrived,
    load_sem, send_sem, recv_sem, swap_send, swap_recv,
):
    count = major * minor
    me = lax.axis_index("patch")
    mine = lax.axis_index("head")
    a, b = me // minor, me % minor
    strip_rows = stale_hbm.shape[0]
    lat_rows = q_hbm.shape[1]
    text_rows = strip_rows - lat_rows
    feats = q_hbm.shape[2]
    width = w_hbm.shape[1]
    col_width = hid_hbm.shape[1]
    out_rows = lat_rows // heads_split
    sides = (
        (a > 0, me - minor), (a < major - 1, me + minor),
        (b > 0, me - 1), (b < minor - 1, me + 1),
    )
    if minor == 1:
        sides = sides[:2]

    loads = [
        pltpu.make_async_copy(step_hbm, own_v, load_sem.at[0]),
        pltpu.make_async_copy(q_hbm, q_v, load_sem.at[1]),
        pltpu.make_async_copy(hid_hbm, hid_v, load_sem.at[2]),
        pltpu.make_async_copy(gate_hbm, gate_v, load_sem.at[3]),
        pltpu.make_async_copy(w_hbm, w_v, load_sem.at[4]),
    ]
    barrier = pltpu.get_barrier_semaphore()
    greeted = heads_split - 1
    for there, index in sides:
        greeted = greeted + there.astype(jnp.int32)

        @pl.when(there)
        def _():
            pl.semaphore_signal(barrier, inc=1, device_id={"patch": index}, device_id_type=MESH_ID)

    for k in range(1, heads_split):
        pl.semaphore_signal(
            barrier, inc=1, device_id={"head": (mine + k) % heads_split}, device_id_type=MESH_ID
        )
    for load in loads:
        load.start()
    pl.semaphore_wait(barrier, greeted)

    def remote(source, block, piece, side):
        return pltpu.make_async_remote_copy(
            src_ref=source,
            dst_ref=slots.at[block, piece],
            send_sem=send_sem.at[block, piece, side],
            recv_sem=recv_sem.at[block, piece],
            device_id={"patch": sides[side][1]},
            device_id_type=MESH_ID,
        )

    def spread(source, block, piece, to):
        for side in to:
            if side < len(sides):
                @pl.when(sides[side][0])
                def _():
                    remote(source, block, piece, side).start()

    def drain(block, piece, to):
        for side in to:
            if side < len(sides):
                @pl.when(sides[side][0])
                def _():
                    remote(slots.at[block, piece], block, piece, side).wait_send()

    def landed(block, piece):
        remote(slots.at[block, piece], block, piece, 0).wait_recv()

    own_source = (stale_hbm, step_hbm.at[0])
    for piece in range(2):
        spread(own_source[piece], me, piece, (0, 1, 2, 3))

    def clear(p, carry):
        rows = pl.ds(pl.multiple_of(p * PAD, PAD), PAD)
        for s in range(2):
            for kind in range(2):
                padded[s, kind, rows, :] = jnp.zeros((PAD, feats), jnp.bfloat16)
        return carry

    lax.fori_loop(0, count, clear, 0)

    def fill(block, s, source):
        rows = pl.ds(pl.multiple_of(block * PAD, PAD), strip_rows)
        both = source[...]
        for kind in range(2):
            padded[s, kind, rows, :] = both[:, kind, :]

    loads[3].wait()
    plan_rows = lax.broadcasted_iota(jnp.int32, gate_v.shape, 0)
    table = gate_v[...].astype(jnp.float32)
    gates = [
        jnp.sum(jnp.where(plan_rows == t_ref[s], table, 0.0), axis=0, keepdims=True)
        for s in range(2)
    ]
    loads[0].wait()
    for s in range(2):
        fill(me, s, own_v.at[s])

    def cross(t, piece):
        for away in {0: (a,)}.get(t, (a - t, a + t)):
            @pl.when((away >= 0) & (away < major))
            def _():
                block = away * minor + (1 - b)
                landed(block, piece)
                fill(block, piece, slots.at[block, piece])

    for t in range(1, major):
        steps = ((a - t, 1), (a + t, 0))
        for piece in range(2):
            for away, onward in steps:
                @pl.when((away >= 0) & (away < major))
                def _():
                    block = away * minor + b
                    landed(block, piece)
                    spread(slots.at[block, piece], block, piece, (onward, 2, 3))

        for piece in range(2):
            for away, onward in steps:
                @pl.when((away >= 0) & (away < major))
                def _():
                    block = away * minor + b
                    fill(block, piece, slots.at[block, piece])

            if minor == 2:
                cross(t - 1, piece)

    if minor > 2:
        for u in range(1, minor):
            for away, onward in ((b - u, 3), (b + u, 2)):
                @pl.when((away >= 0) & (away < minor))
                def _():
                    def one(r, carry):
                        block = r * minor + away
                        for piece in range(2):
                            landed(block, piece)
                            if u < minor - 1:
                                spread(slots.at[block, piece], block, piece, (onward,))
                            fill(block, piece, slots.at[block, piece])
                        return carry

                    lax.fori_loop(0, major, one, 0)

    loads[1].wait()

    keys = count * PAD
    place = lax.broadcasted_iota(jnp.int32, (1, keys), 1)
    holder, within = place // PAD, place % PAD
    usable = (within < lat_rows) | (
        (within < strip_rows) & (holder * text_rows + within - lat_rows < len_ref[0])
    )
    heads = [slice(h * HDIM, (h + 1) * HDIM) for h in range(feats // HDIM)]

    def attend(s):
        scores = jnp.concatenate(
            [
                lax.dot_general(
                    q_v[s, :, cols], padded[s, 0, :, cols], (((1,), (1,)), ((), ())),
                    preferred_element_type=jnp.float32,
                )
                for cols in heads
            ],
            axis=0,
        ) * (1.0 / HDIM**0.5)
        scores = jnp.where(usable, scores, jnp.float32(-1e30))
        top = jnp.max(scores, axis=1, keepdims=True)
        expo = jnp.exp(scores - top)
        weights = (expo * (1.0 / jnp.sum(expo, axis=1, keepdims=True))).astype(jnp.bfloat16)
        parts = [
            jnp.dot(
                weights[h * lat_rows:(h + 1) * lat_rows], padded[s, 1, :, cols],
                preferred_element_type=jnp.float32,
            ).astype(jnp.bfloat16)
            for h, cols in enumerate(heads)
        ]
        return jnp.concatenate(parts, axis=1)

    chunks = 2 * heads_split
    chunk = width // chunks
    swaps = []
    for s in range(2):
        if minor == 2:
            cross(major - 1, s)
        mixed = attend(s)
        if s == 0:
            loads[2].wait()
            loads[4].wait()
        for c in range(chunks):
            cols = slice(c * chunk, (c + 1) * chunk)
            term = gates[s][:, cols] * jnp.dot(
                mixed, w_v[:, cols], preferred_element_type=jnp.float32
            )
            if s == 0:
                owner, inner = (c * chunk) // col_width, (c * chunk) % col_width
                base = hid_v[:, inner:inner + chunk].astype(jnp.float32)
                partial[:, cols] = jnp.where(mine == owner, base, 0.0) + term
            else:
                partial[:, cols] = partial[:, cols] + term
                for k in range(1, heads_split):
                    peer = (mine + k) % heads_split
                    swap = pltpu.make_async_remote_copy(
                        src_ref=partial.at[pl.ds(pl.multiple_of(peer * out_rows, out_rows), out_rows), pl.ds(c * chunk, chunk)],
                        dst_ref=arrived.at[k - 1, :, pl.ds(c * chunk, chunk)],
                        send_sem=swap_send.at[k - 1, c],
                        recv_sem=swap_recv.at[k - 1, c],
                        device_id={"head": peer},
                        device_id_type=MESH_ID,
                    )
                    swap.start()
                    swaps.append((c, k, swap))

    own = pl.ds(pl.multiple_of(mine * out_rows, out_rows), out_rows)
    for c in range(chunks):
        cols = slice(c * chunk, (c + 1) * chunk)
        total = partial[own, cols]
        for cc, k, swap in swaps:
            if cc == c:
                swap.wait_recv()
                total = total + arrived[k - 1, :, cols]
        out_ref[:, cols] = total.astype(out_ref.dtype)

    for _, _, swap in swaps:
        swap.wait_send()
    for piece in range(2):
        drain(me, piece, (0, 1, 2, 3))
    for t in range(1, major):
        for piece in range(2):
            for away, onward in ((a - t, 1), (a + t, 0)):
                @pl.when((away >= 0) & (away < major))
                def _():
                    drain(away * minor + b, piece, (onward, 2, 3))
    for u in range(1, minor - 1):
        for away, onward in ((b - u, 3), (b + u, 2)):
            @pl.when((away >= 0) & (away < minor))
            def _():
                def one(r, carry):
                    for piece in range(2):
                        drain(r * minor + away, piece, (onward,))
                    return carry

                lax.fori_loop(0, major, one, 0)


def per_device(major, minor, heads_split, queries, stale_pairs, step_pairs, hidden, out_weight, gate_table, t_index, text_len):
    count = major * minor
    stale_pairs = jnp.transpose(stale_pairs, (1, 0, 2))
    step_pairs = jnp.transpose(step_pairs, (0, 2, 1, 3))
    lat_rows, feats = queries.shape[1:]
    width = out_weight.shape[1]
    out_rows = lat_rows // heads_split
    chunks = 2 * heads_split
    anywhere = pl.BlockSpec(memory_space=pl.ANY)
    scalars = pl.BlockSpec(memory_space=pltpu.SMEM)
    return pl.pallas_call(
        functools.partial(kernel, major, minor, heads_split),
        out_shape=jax.ShapeDtypeStruct((out_rows, width), jnp.bfloat16),
        in_specs=[scalars] * 2 + [anywhere] * 6,
        out_specs=pl.BlockSpec(memory_space=pltpu.VMEM),
        scratch_shapes=[
            pltpu.VMEM((count,) + step_pairs.shape, jnp.bfloat16),
            pltpu.VMEM(step_pairs.shape, jnp.bfloat16),
            pltpu.VMEM((2, 2, count * PAD, feats), jnp.bfloat16),
            pltpu.VMEM(out_weight.shape, jnp.bfloat16),
            pltpu.VMEM(queries.shape, jnp.bfloat16),
            pltpu.VMEM(hidden.shape, jnp.bfloat16),
            pltpu.VMEM(gate_table.shape, jnp.bfloat16),
            pltpu.VMEM((lat_rows, width), jnp.float32),
            pltpu.VMEM((heads_split - 1, out_rows, width), jnp.float32),
            pltpu.SemaphoreType.DMA((5,)),
            pltpu.SemaphoreType.DMA((count, 2, 4)),
            pltpu.SemaphoreType.DMA((count, 2)),
            pltpu.SemaphoreType.DMA((heads_split - 1, chunks)),
            pltpu.SemaphoreType.DMA((heads_split - 1, chunks)),
        ],
        compiler_params=pltpu.CompilerParams(collective_id=0, has_side_effects=True),
        name="block",
    )(t_index, text_len, queries, stale_pairs, step_pairs, hidden, out_weight, gate_table)


def solution(mesh):
    minor = minor_extent(mesh)
    return jax.shard_map(
        functools.partial(per_device, mesh.shape["patch"] // minor, minor, mesh.shape["head"]),
        mesh=mesh,
        in_specs=(
            P(None, ("groups", "patch"), "head"),
            P(None, ("groups", "patch"), "head"),
            P(None, None, ("groups", "patch"), "head"),
            P(("groups", "patch"), "head"),
            P("head", None),
            P(),
            P("groups"),
            P("groups"),
        ),
        out_specs=P(("groups", "patch", "head"), None),
        check_vma=False,
    )
```

```python
import functools

import jax
import jax.numpy as jnp
from jax import lax
from jax.experimental import pallas as pl
from jax.experimental.pallas import tpu as pltpu
from jax.sharding import PartitionSpec as P

HDIM = 128
PAD = 32
MESH_ID = pl.DeviceIdType.MESH


def minor_extent(mesh):
    names = list(mesh.axis_names)
    order = [names.index("patch")] + [i for i, name in enumerate(names) if name != "patch"]
    line = mesh.devices.transpose(order).reshape(mesh.shape["patch"], -1)[:, 0]
    count = len(line)
    try:
        spots = [tuple(device.coords) for device in line]
    except AttributeError:
        return 2 if count % 2 == 0 else 1
    varying = lambda spot: [i for i in range(len(spot)) if spot[i] != spots[0][i]]
    extent = 1
    while extent < count and varying(spots[extent]) == varying(spots[1]) and len(varying(spots[1])) == 1:
        extent += 1
    return extent if count % extent == 0 else 1


def kernel(
    major, minor, heads_split,
    t_ref, len_ref, q_hbm, stale_hbm, step_hbm, hid_hbm, w_hbm, gate_hbm,
    out_ref,
    slots, own_v, padded, w_v, q_v, hid_v, gate_v, partial, arrived,
    load_sem, send_sem, recv_sem, swap_send, swap_recv,
):
    count = major * minor
    me = lax.axis_index("patch")
    mine = lax.axis_index("head")
    a, b = me // minor, me % minor
    strip_rows = stale_hbm.shape[0]
    lat_rows = q_hbm.shape[1]
    text_rows = strip_rows - lat_rows
    feats = q_hbm.shape[2]
    width = w_hbm.shape[1]
    col_width = hid_hbm.shape[1]
    out_rows = lat_rows // heads_split
    sides = (
        (a > 0, me - minor), (a < major - 1, me + minor),
        (b > 0, me - 1), (b < minor - 1, me + 1),
    )
    if minor == 1:
        sides = sides[:2]

    loads = [
        pltpu.make_async_copy(step_hbm, own_v, load_sem.at[0]),
        pltpu.make_async_copy(q_hbm, q_v, load_sem.at[1]),
        pltpu.make_async_copy(hid_hbm, hid_v, load_sem.at[2]),
        pltpu.make_async_copy(gate_hbm, gate_v, load_sem.at[3]),
        pltpu.make_async_copy(w_hbm, w_v, load_sem.at[4]),
    ]
    barrier = pltpu.get_barrier_semaphore()
    greeted = heads_split - 1
    for there, index in sides:
        greeted = greeted + there.astype(jnp.int32)

        @pl.when(there)
        def _():
            pl.semaphore_signal(barrier, inc=1, device_id={"patch": index}, device_id_type=MESH_ID)

    for k in range(1, heads_split):
        pl.semaphore_signal(
            barrier, inc=1, device_id={"head": (mine + k) % heads_split}, device_id_type=MESH_ID
        )
    for load in loads:
        load.start()
    pl.semaphore_wait(barrier, greeted)

    def remote(source, block, piece, side):
        return pltpu.make_async_remote_copy(
            src_ref=source,
            dst_ref=slots.at[block, piece],
            send_sem=send_sem.at[block, piece, side],
            recv_sem=recv_sem.at[block, piece],
            device_id={"patch": sides[side][1]},
            device_id_type=MESH_ID,
        )

    def spread(source, block, piece, to):
        for side in to:
            if side < len(sides):
                @pl.when(sides[side][0])
                def _():
                    remote(source, block, piece, side).start()

    def drain(block, piece, to):
        for side in to:
            if side < len(sides):
                @pl.when(sides[side][0])
                def _():
                    remote(slots.at[block, piece], block, piece, side).wait_send()

    def landed(block, piece):
        remote(slots.at[block, piece], block, piece, 0).wait_recv()

    own_source = (stale_hbm, step_hbm.at[0])
    for piece in range(2):
        spread(own_source[piece], me, piece, (0, 1, 2, 3))

    def clear(p, carry):
        rows = pl.ds(pl.multiple_of(p * PAD, PAD), PAD)
        for s in range(2):
            for kind in range(2):
                padded[s, kind, rows, :] = jnp.zeros((PAD, feats), jnp.bfloat16)
        return carry

    lax.fori_loop(0, count, clear, 0)

    def fill(block, s, source):
        rows = pl.ds(pl.multiple_of(block * PAD, PAD), strip_rows)
        both = source[...]
        for kind in range(2):
            padded[s, kind, rows, :] = both[:, kind, :]

    loads[3].wait()
    plan_rows = lax.broadcasted_iota(jnp.int32, gate_v.shape, 0)
    table = gate_v[...].astype(jnp.float32)
    gates = [
        jnp.sum(jnp.where(plan_rows == t_ref[s], table, 0.0), axis=0, keepdims=True)
        for s in range(2)
    ]
    loads[0].wait()
    for s in range(2):
        fill(me, s, own_v.at[s])

    def cross(t, piece):
        for away in {0: (a,)}.get(t, (a - t, a + t)):
            @pl.when((away >= 0) & (away < major))
            def _():
                block = away * minor + (1 - b)
                landed(block, piece)
                fill(block, piece, slots.at[block, piece])

    for t in range(1, major):
        steps = ((a - t, 1), (a + t, 0))
        for piece in range(2):
            for away, onward in steps:
                @pl.when((away >= 0) & (away < major))
                def _():
                    block = away * minor + b
                    landed(block, piece)
                    spread(slots.at[block, piece], block, piece, (onward, 2, 3))

        for piece in range(2):
            for away, onward in steps:
                @pl.when((away >= 0) & (away < major))
                def _():
                    block = away * minor + b
                    fill(block, piece, slots.at[block, piece])

            if minor == 2:
                cross(t - 1, piece)

    if minor > 2:
        for u in range(1, minor):
            for away, onward in ((b - u, 3), (b + u, 2)):
                @pl.when((away >= 0) & (away < minor))
                def _():
                    def one(r, carry):
                        block = r * minor + away
                        for piece in range(2):
                            landed(block, piece)
                            if u < minor - 1:
                                spread(slots.at[block, piece], block, piece, (onward,))
                            fill(block, piece, slots.at[block, piece])
                        return carry

                    lax.fori_loop(0, major, one, 0)

    loads[1].wait()

    keys = count * PAD
    place = lax.broadcasted_iota(jnp.int32, (1, keys), 1)
    holder, within = place // PAD, place % PAD
    usable = (within < lat_rows) | (
        (within < strip_rows) & (holder * text_rows + within - lat_rows < len_ref[0])
    )
    heads = [slice(h * HDIM, (h + 1) * HDIM) for h in range(feats // HDIM)]

    def attend(s):
        scores = jnp.concatenate(
            [
                lax.dot_general(
                    q_v[s, :, cols], padded[s, 0, :, cols], (((1,), (1,)), ((), ())),
                    preferred_element_type=jnp.float32,
                )
                for cols in heads
            ],
            axis=0,
        ) * (1.0 / HDIM**0.5)
        scores = jnp.where(usable, scores, jnp.float32(-1e30))
        top = jnp.max(scores, axis=1, keepdims=True)
        expo = jnp.exp(scores - top)
        weights = (expo * (1.0 / jnp.sum(expo, axis=1, keepdims=True))).astype(jnp.bfloat16)
        parts = [
            jnp.dot(
                weights[h * lat_rows:(h + 1) * lat_rows], padded[s, 1, :, cols],
                preferred_element_type=jnp.float32,
            ).astype(jnp.bfloat16)
            for h, cols in enumerate(heads)
        ]
        return jnp.concatenate(parts, axis=1)

    chunks = heads_split
    chunk = width // chunks
    swaps = []
    for s in range(2):
        if minor == 2:
            cross(major - 1, s)
        mixed = attend(s)
        if s == 0:
            loads[2].wait()
            loads[4].wait()
        for c in range(chunks):
            cols = slice(c * chunk, (c + 1) * chunk)
            term = gates[s][:, cols] * jnp.dot(
                mixed, w_v[:, cols], preferred_element_type=jnp.float32
            )
            if s == 0:
                owner, inner = (c * chunk) // col_width, (c * chunk) % col_width
                base = hid_v[:, inner:inner + chunk].astype(jnp.float32)
                partial[:, cols] = jnp.where(mine == owner, base, 0.0) + term
            else:
                partial[:, cols] = partial[:, cols] + term
    for k in range(1, heads_split):
        peer = (mine + k) % heads_split
        swap = pltpu.make_async_remote_copy(
            src_ref=partial.at[pl.ds(pl.multiple_of(peer * out_rows, out_rows), out_rows)],
            dst_ref=arrived.at[k - 1],
            send_sem=swap_send.at[k - 1],
            recv_sem=swap_recv.at[k - 1],
            device_id={"head": peer},
            device_id_type=MESH_ID,
        )
        swap.start()
        swaps.append(swap)

    own = pl.ds(pl.multiple_of(mine * out_rows, out_rows), out_rows)
    total = partial[own]
    for k, swap in enumerate(swaps):
        swap.wait_recv()
        total = total + arrived[k]
    out_ref[...] = total.astype(out_ref.dtype)

    for swap in swaps:
        swap.wait_send()
    for piece in range(2):
        drain(me, piece, (0, 1, 2, 3))
    for t in range(1, major):
        for piece in range(2):
            for away, onward in ((a - t, 1), (a + t, 0)):
                @pl.when((away >= 0) & (away < major))
                def _():
                    drain(away * minor + b, piece, (onward, 2, 3))
    for u in range(1, minor - 1):
        for away, onward in ((b - u, 3), (b + u, 2)):
            @pl.when((away >= 0) & (away < minor))
            def _():
                def one(r, carry):
                    for piece in range(2):
                        drain(r * minor + away, piece, (onward,))
                    return carry

                lax.fori_loop(0, major, one, 0)


def per_device(major, minor, heads_split, queries, stale_pairs, step_pairs, hidden, out_weight, gate_table, t_index, text_len):
    count = major * minor
    stale_pairs = jnp.transpose(stale_pairs, (1, 0, 2))
    step_pairs = jnp.transpose(step_pairs, (0, 2, 1, 3))
    lat_rows, feats = queries.shape[1:]
    width = out_weight.shape[1]
    out_rows = lat_rows // heads_split
    anywhere = pl.BlockSpec(memory_space=pl.ANY)
    scalars = pl.BlockSpec(memory_space=pltpu.SMEM)
    return pl.pallas_call(
        functools.partial(kernel, major, minor, heads_split),
        out_shape=jax.ShapeDtypeStruct((out_rows, width), jnp.bfloat16),
        in_specs=[scalars] * 2 + [anywhere] * 6,
        out_specs=pl.BlockSpec(memory_space=pltpu.VMEM),
        scratch_shapes=[
            pltpu.VMEM((count,) + step_pairs.shape, jnp.bfloat16),
            pltpu.VMEM(step_pairs.shape, jnp.bfloat16),
            pltpu.VMEM((2, 2, count * PAD, feats), jnp.bfloat16),
            pltpu.VMEM(out_weight.shape, jnp.bfloat16),
            pltpu.VMEM(queries.shape, jnp.bfloat16),
            pltpu.VMEM(hidden.shape, jnp.bfloat16),
            pltpu.VMEM(gate_table.shape, jnp.bfloat16),
            pltpu.VMEM((lat_rows, width), jnp.float32),
            pltpu.VMEM((heads_split - 1, out_rows, width), jnp.float32),
            pltpu.SemaphoreType.DMA((5,)),
            pltpu.SemaphoreType.DMA((count, 2, 4)),
            pltpu.SemaphoreType.DMA((count, 2)),
            pltpu.SemaphoreType.DMA((heads_split - 1,)),
            pltpu.SemaphoreType.DMA((heads_split - 1,)),
        ],
        compiler_params=pltpu.CompilerParams(collective_id=0, has_side_effects=True),
        name="block",
    )(t_index, text_len, queries, stale_pairs, step_pairs, hidden, out_weight, gate_table)


def solution(mesh):
    minor = minor_extent(mesh)
    return jax.shard_map(
        functools.partial(per_device, mesh.shape["patch"] // minor, minor, mesh.shape["head"]),
        mesh=mesh,
        in_specs=(
            P(None, ("groups", "patch"), "head"),
            P(None, ("groups", "patch"), "head"),
            P(None, None, ("groups", "patch"), "head"),
            P(("groups", "patch"), "head"),
            P("head", None),
            P(),
            P("groups"),
            P("groups"),
        ),
        out_specs=P(("groups", "patch", "head"), None),
        check_vma=False,
    )
```
